32 devices in a mesh: tok: 16 (over z, x, core), lyr: 2 (over y).
Axes of the slice: x: 2, y: 2, z: 4, core: 2. Of those that a mesh axis runs over, the one named last changes fastest.
Arguments:
- feature_codes: bfloat16 [4, 2048, 2, 256], P('lyr', 'tok'), may hold values from 0 to 21, as said below
- block_ids: int32 [4, 2048, 2], P('lyr', 'tok'), may hold values from 0 to 31, all different within a row; in each aligned block of 128 rows (0 to 127, 128 to 255, ..., all dimensions but the last counted through in order) at most 16 rows name the same one
- target_layer: int32 [2048], P('tok'), may hold values from 0 to 3
- request_ids: int32 [2048], P('tok'), may hold values from 0 to 15
- target_resid: bfloat16 [2048, 2304], P('tok'), may hold values from -6 to 6
- decoder: bfloat16 [4, 8192, 2304], P('lyr', 'tok'), may hold values from -0.25 to 0.25
Outputs:
- scores: bfloat16 [4, 2048, 2, 256], P('lyr', 'tok')
- request_totals: float32 [16, 4, 8192], P(None, 'lyr', 'tok')
The draws below stay inside these ranges and needn't reach their ends.
Inputs may be any that keep to these rules, and one draw needn't show every extreme that they name: `block_ids`: the 2 panel indices of one token at one source layer are distinct; among the 128 tokens of one index of tok at one source layer no panel is named by more than 16 of them, a bound that some block reaches. `feature_codes`: nonnegative, with many entries zero.
All inputs are finite; a program needn't handle non-finite values.
Results may differ from the reference program's by a relative error of at most 0.0053.
Values may be sent and summed in bfloat16 or wider, within the bound.
A program may use at most 64 MiB of HBM per device.

```python
import math
import jax
import jax.numpy as jnp
import numpy as np
from jax import lax

D = 2304
PANEL = 256
PANELS = 32
KACT = 2
REQUESTS = 16
TOK_DEV = 128
CAP = 16
F = 8192
LAYERS = 4
TOKENS = 2048
N_TOK = 16


def draw_feature_codes(key, part):
    normal_key, scale_key = jax.random.split(jax.random.fold_in(key, 17))
    normal_part = jax.random.normal(normal_key, (LAYERS, TOKENS, KACT, PANEL), jnp.float32)
    spread = jnp.exp(jax.random.uniform(scale_key, (LAYERS, TOKENS, KACT, 1), jnp.float32, jnp.log(0.5), jnp.log(2.0)))
    return (jnp.clip(normal_part, 0.0, 5.0) * spread).astype(jnp.bfloat16)


def touch_ends(array, rng, least, high):
    dims = array.shape
    spot = [jax.random.randint(jax.random.fold_in(rng, axis), (), 0, dims[axis]) for axis in range(len(dims))]
    array = array.at[tuple(spot)].set(least)
    longest = dims.index(max(dims))
    spot[longest] = (spot[longest] + 1) % dims[longest]
    return array.at[tuple(spot)].set(high)


def block_scale(key, dims, pieces, low, largest):
    level = 1.0
    for position, parts in pieces:
        draws = jax.random.uniform(jax.random.fold_in(jax.random.fold_in(key, 6), position), (parts,), jnp.float32, low / len(pieces), largest / len(pieces))
        level = level * jnp.repeat(jnp.exp(draws), dims[position] // parts).reshape((-1,) + (1,) * (len(dims) - 1 - position))
    return level


def shared_out(stream_key, own, number, rows, count, top, bound, slope):
    sequence = jax.random.permutation(stream_key, count)
    heavy_load, usual = shares(count, rows * top, bound, slope, True), shares(count, rows * top, bound, slope, False)
    places = jnp.arange(count)

    def named(sizes, turn):
        used = int((sizes > 0).sum())
        fixed = max(1, used // 4)
        passed = fixed + (places - fixed + turn * (used - fixed)) % max(1, count - fixed)
        return jnp.zeros((count,), jnp.int32).at[sequence[jnp.where(places < fixed, places, passed)]].set(jnp.asarray(sizes, jnp.int32))

    sizes = jnp.where(number % 4 == 0, named(heavy_load, number // 4), named(usual, number - number // 4 - 1))
    mixed = jax.random.permutation(jax.random.fold_in(own, 3), count)
    giver, sink = mixed[0:count // 2 * 2:2], mixed[1:count // 2 * 2:2]
    margin = jnp.minimum(sizes[giver] - 1, bound - sizes[sink]) // 2
    margin = jnp.where((giver == sequence[0]) | (sink == sequence[0]) | (sizes[sink] == 0), 0, jnp.maximum(margin, 0))
    passed = jax.random.randint(jax.random.fold_in(own, 4), (count // 2,), 0, 1 << 20) % (margin + 1)
    sizes = sizes.at[giver].add(-passed).at[sink].add(passed)
    items = jnp.searchsorted(jnp.cumsum(sizes), jnp.arange(rows * top), side="right").astype(jnp.int32)
    table = items.reshape(top, rows).T
    table = table[jax.random.permutation(jax.random.fold_in(own, 1), rows)]
    turn = jax.random.randint(jax.random.fold_in(own, 2), (rows, 1), 0, top)
    return jnp.take_along_axis(table, (jnp.arange(top)[None, :] + turn) % top, axis=1)


def shares(amount, total, limit, skew, full):
    loads = [(1 << 20) // math.isqrt(rank ** skew) + 1 for rank in range(1, amount + 1)]
    largest = limit if full else min(limit, max(-(-total // amount), total * loads[0] // sum(loads)))
    least = 1 if total - largest >= amount - 1 else 0
    holding, rest = [largest] + [least] * (amount - 1), total - largest - least * (amount - 1)
    while rest > 0:
        free = [i for i in range(1, amount) if holding[i] < largest] or [i for i in range(1, amount) if holding[i] < limit]
        whole, remaining = sum([loads[i] for i in free]), rest
        for i in free:
            extra = min(limit - holding[i], max(1, remaining * loads[i] // whole), rest)
            holding[i] = holding[i] + extra
            rest = rest - extra
    return np.array(holding)


def bell_draw(stream_key, dims, scale, most, pieces=(), held_as=jnp.bfloat16):
    drawn = jax.random.normal(stream_key, dims, jnp.float32) * scale
    if len(pieces) > 0:
        drawn = block_scale(stream_key, dims, pieces, -0.22, 0.18) * drawn
    return jnp.clip(drawn, min=-most, max=most).astype(held_as)


def setup_inputs(seed: int = 0) -> dict:
    arg_keys = jax.random.split(jax.random.key(seed), 7)
    feature_codes = draw_feature_codes(jax.random.fold_in(arg_keys[6], 71), 0)
    block_ids_keys = jax.random.split(jax.random.fold_in(arg_keys[1], 1), LAYERS * TOKENS // TOK_DEV)
    block_ids_turns = jax.random.permutation(jax.random.fold_in(arg_keys[1], 3), LAYERS * TOKENS // TOK_DEV)
    block_ids = jax.vmap(lambda own, number: shared_out(jax.random.fold_in(arg_keys[1], 2), own, number, TOK_DEV, PANELS, KACT, CAP, 1))(block_ids_keys, block_ids_turns).reshape((LAYERS, TOKENS, KACT))
    target_layer = touch_ends(jax.random.randint(arg_keys[2], (TOKENS,), 0, LAYERS), jax.random.fold_in(arg_keys[2], 1), 0, LAYERS - 1).astype(jnp.int32)
    request_ids = touch_ends(jax.random.randint(arg_keys[3], (TOKENS,), 0, REQUESTS), jax.random.fold_in(arg_keys[3], 1), 0, REQUESTS - 1).astype(jnp.int32)
    target_resid = bell_draw(arg_keys[4], (TOKENS, D), 1.0, 6.0, ((0, 16),))
    decoder = bell_draw(arg_keys[5], (LAYERS, F, D), (KACT * PANEL) ** -0.5, 0.25, ((0, 2), (1, 16)))
    return dict(feature_codes=feature_codes, block_ids=block_ids, target_layer=target_layer, request_ids=request_ids, target_resid=target_resid, decoder=decoder)


def grouped(sorted_rows, weights, counts, starts, width):
    window_size = N_TOK * CAP
    total_rows = sorted_rows.shape[0]
    positions = jnp.arange(window_size, dtype=jnp.int32)

    def add_panel(buffer, panel_index):
        offset = starts[panel_index]
        window = lax.dynamic_slice_in_dim(sorted_rows, offset, window_size, 0)
        product = jnp.dot(window, weights[panel_index], preferred_element_type=jnp.float32)
        rounded = lax.optimization_barrier(product.astype(jnp.bfloat16)).astype(jnp.float32)
        keeping = positions < counts[panel_index]
        rounded = jnp.where(keeping[:, None], rounded, jnp.zeros_like(rounded))
        current = lax.dynamic_slice_in_dim(buffer, offset, window_size, 0)
        buffer = lax.dynamic_update_slice_in_dim(buffer, current + rounded, offset, 0)
        return (buffer, None)
    initial = jnp.zeros((total_rows, width), jnp.float32)
    buffer, _ = lax.scan(add_panel, initial, jnp.arange(PANELS, dtype=jnp.int32))
    return buffer[:total_rows - window_size]

def reference(feature_codes, block_ids, target_layer, request_ids, target_resid, decoder):
    count = target_resid.shape[0]
    row_total = count * KACT
    window_size = N_TOK * CAP
    panel_iota = jnp.arange(PANELS, dtype=jnp.int32)
    row_iota = jnp.arange(row_total, dtype=jnp.int32)
    rebuilt = jnp.zeros((count, D), jnp.float32)
    saved = []
    for source in range(LAYERS):
        alive_mask = (target_layer >= source).astype(feature_codes.dtype)
        masked = feature_codes[source] * alive_mask[:, None, None]
        flat_ids = block_ids[source].reshape(row_total).astype(jnp.int32)
        ranking = jnp.argsort(flat_ids, stable=True).astype(jnp.int32)
        inverse = jnp.zeros((row_total,), jnp.int32).at[ranking].set(row_iota)
        counts = lax.optimization_barrier(jnp.sum((flat_ids[:, None] == panel_iota[None, :]).astype(jnp.int32), axis=0)).astype(jnp.int32)
        starts = (jnp.cumsum(counts) - counts).astype(jnp.int32)
        code_rows = masked.reshape(row_total, PANEL)[ranking]
        code_rows = jnp.concatenate([code_rows, jnp.zeros((window_size, PANEL), code_rows.dtype)], axis=0)
        panels = decoder[source].reshape(PANELS, PANEL, D)
        contrib = grouped(code_rows, panels, counts, starts, D)[inverse]
        rebuilt = rebuilt + lax.optimization_barrier(jnp.sum(contrib.reshape(count, KACT, D), axis=1))
        saved.append((masked, ranking, inverse, counts, starts))
    error = target_resid.astype(jnp.float32) - rebuilt
    spread = lax.optimization_barrier(jnp.mean(error * error, axis=-1, keepdims=True))
    gradient = (error * lax.rsqrt(spread + 1e-06)).astype(jnp.bfloat16)
    members = (request_ids[:, None] == jnp.arange(REQUESTS, dtype=jnp.int32)[None, :]).astype(jnp.float32)
    scores = []
    totals = []
    for source in range(LAYERS):
        masked, ranking, inverse, counts, starts = saved[source]
        token_of = ranking // KACT
        grad_rows = jnp.concatenate([gradient[token_of], jnp.zeros((window_size, D), gradient.dtype)], axis=0)
        panels_t = jnp.swapaxes(decoder[source].reshape(PANELS, PANEL, D), 1, 2)
        projected = grouped(grad_rows, panels_t, counts, starts, PANEL)[inverse].reshape(count, KACT, PANEL)
        attribution = masked.astype(jnp.float32) * projected
        scores.append(attribution.astype(jnp.bfloat16))
        summed = jnp.zeros((REQUESTS * PANELS, PANEL), jnp.float32)
        for which in range(KACT):
            panel_hot = (block_ids[source][:, which][:, None] == panel_iota[None, :]).astype(jnp.float32)
            combined = (members[:, :, None] * panel_hot[:, None, :]).reshape(count, REQUESTS * PANELS)
            summed = summed + jnp.dot(combined.T, attribution[:, which], precision=lax.Precision.HIGHEST)
        totals.append(summed.reshape(REQUESTS, PANELS * PANEL))
    return (jnp.stack(scores, axis=0), jnp.stack(totals, axis=1))
```

```python
import functools

import jax
import jax.numpy as jnp
from jax import lax
from jax.experimental import pallas as pl
from jax.experimental.pallas import tpu as pltpu
from jax.sharding import PartitionSpec as P

REQUESTS = 16
CAP = 16
WAVES = 2
MESH = pl.DeviceIdType.MESH


class Place:
    def __init__(self):
        tok, y = lax.axis_index("tok"), lax.axis_index("lyr")
        z, x, c = tok // 4, (tok // 2) % 2, tok % 2
        self.z, self.c = z, c
        self.inner = (z % 3) != 0
        self.first = (1 - c) * y + c * x
        self.second = (1 - c) * x + c * y
        across_x, across_y = (tok + 2 - 4 * x, y), (tok, 1 - y)
        self.to_first = tuple((1 - c) * a + c * b for a, b in zip(across_y, across_x))
        self.to_second = tuple((1 - c) * a + c * b for a, b in zip(across_x, across_y))
        self.to_core = (tok + 1 - 2 * c, y)
        self.tok, self.y = tok, y
        half = z // 2
        self.near = [z, z + 1 - 2 * (z % 2), 2 - half, 3 - 3 * half]

    def along(self, step):
        return (self.tok + 4 * step, self.y)

    def quarter(self, first, second):
        return (1 - self.c) * (second * 2 + first) + self.c * (first * 2 + second)

    def peer(self, distance):
        return ((self.tok + distance) % 16, self.y)

    def greet(self):
        gate = pltpu.get_barrier_semaphore()
        for distance in range(1, 16):
            pl.semaphore_signal(gate, inc=1, device_id=self.peer(distance), device_id_type=MESH)
        pl.semaphore_signal(gate, inc=1, device_id=(self.tok, 1 - self.y), device_id_type=MESH)

    def meet(self):
        pl.semaphore_wait(pltpu.get_barrier_semaphore(), 16)


def remote(src, dst, send, recv, target):
    return pltpu.make_async_remote_copy(
        src_ref=src, dst_ref=dst, send_sem=send, recv_sem=recv, device_id=target, device_id_type=MESH
    )


def f32(value):
    return value.astype(jnp.float32)


def ones(where):
    return jnp.where(where, 1.0, 0.0).astype(jnp.bfloat16)


def rows_of(shape):
    return lax.broadcasted_iota(jnp.int32, shape, 0)


def lanes_of(shape):
    return lax.broadcasted_iota(jnp.int32, shape, 1)


def product(left, right, left_dim=1, right_dim=0):
    return lax.dot_general(left, right, (((left_dim,), (right_dim,)), ((), ())), preferred_element_type=jnp.float32)


def transcoder_kernel(
    codes_ref, ids_ref, request_ref, limit_ref, decoder_ref, target_ref, scores_ref, totals_ref,
    weights, resid, packed, slot_in, sent, hot, turned, members, core_out, chip_in, held,
    first_out, first_in, second_out, second_in, z_out, z_in, grads, picked, slot_out, slot_back, low,
    load_sem, code_send, code_recv, core_send, core_recv, first_send, first_recv, second_send, second_recv,
    z_send, z_recv, own_core, own_first, own_second, own_z, block_recv, slot_send, slot_recv,
):
    at = Place()
    at.greet()
    half, width = resid.shape
    tokens = limit_ref.shape[1]
    panel = codes_ref.shape[-1]
    slots = 4 * CAP
    step = half // WAVES
    tile = width // 3 if width % 384 == 0 else width
    tiles = [slice(t, t + tile) for t in range(0, width, tile)]
    load = pltpu.make_async_copy(decoder_ref, weights, load_sem.at[0])
    load.start()
    load_target = pltpu.make_async_copy(
        target_ref.at[pl.ds(pl.multiple_of(at.y * half, half), half)], resid, load_sem.at[1]
    )
    load_target.start()

    def wave(w):
        return pl.ds(w * step, step)

    info = []
    ids = ids_ref[...]
    shape = (tokens, tokens)
    earlier = ones(rows_of(shape) < lanes_of(shape))
    panels = rows_of((32, tokens))
    numbers = []
    for layer in (0, 1):
        named = [ids[2 * layer + k : 2 * layer + k + 1] == panels for k in (0, 1)]
        before = product(ones(named[0] | named[1]), earlier)
        alive = limit_ref[...] >= 2 * at.y + layer
        value = None
        for k in (0, 1):
            rank = jnp.sum(jnp.where(named[k], before, 0.0), axis=0, keepdims=True)
            number = f32(ids[2 * layer + k : 2 * layer + k + 1])
            numbers.append((number, rank))
            code = jnp.where(alive, number * CAP + rank, -1.0)
            spot = ones(f32(rows_of((32 * CAP, tokens))) == code)
            sent[2 * layer + k] = spot
            part = product(spot, codes_ref[2 * layer + k])
            value = part if value is None else value + part
        packed[:, layer * 2 * CAP : (layer + 1) * 2 * CAP, :] = value.astype(packed.dtype).reshape(16, 2 * CAP, panel)
    blank = jnp.zeros((7, tokens), jnp.float32)
    info = jnp.concatenate(
        [n for n, _ in numbers] + [r for _, r in numbers] + [f32(request_ref[...]), blank], axis=0
    )
    info = jnp.concatenate([info] * (panel // tokens), axis=1).astype(packed.dtype)
    for target in range(16):
        packed[target, slots : slots + 16, :] = info
    slot_in[at.tok] = packed[at.tok]
    order = (0, 3, 2, 1)

    def peers(j):
        return [at.near[j] * 4 + (at.tok + s) % 4 for s in range(1 if j == 0 else 0, 4)]

    def code_copy(target, source):
        return remote(packed.at[target], slot_in.at[source], code_send.at[target], code_recv.at[source], (target, at.y))

    at.meet()
    for j in order:
        for target in peers(j):
            code_copy(target, at.tok).start()

    eye = ones(rows_of(shape) == lanes_of(shape))

    def unpack(j):
        for source in peers(j):
            code_copy(source, source).wait_recv()

        @pl.loop(0, 4)
        def _(s):
            source = at.near[j] * 4 + s
            told = f32(slot_in[source, slots : slots + 16, :tokens])
            place = [told[i : i + 1] * CAP + told[4 + i : 5 + i] for i in range(4)]
            for away in (0, 1):
                device = at.tok if away == 0 else at.tok + 1 - 2 * at.c
                row = f32(rows_of((2 * CAP, tokens)) + device * (2 * CAP))
                for layer in (0, 1):
                    start = away * slots + layer * 2 * CAP
                    hot[source, start : start + 2 * CAP, :] = ones(
                        (place[2 * layer] == row) | (place[2 * layer + 1] == row)
                    )
            asks = ones(f32(rows_of(shape)) == told[8:9])
            members[source] = product(hot[source, :slots, :], asks, 1, 1).astype(members.dtype)

        for x in (0, 1):
            source = at.near[j] * 4 + x * 2 + at.c
            turned[2 * j + x] = product(hot[source], eye, 0, 0).astype(turned.dtype)

    def panel_span(n):
        return pl.ds(pl.multiple_of(n * CAP, CAP), CAP)

    def weight_span(n):
        return pl.ds(pl.multiple_of(n * panel, panel), panel)

    def core_copy(j, n):
        return remote(
            core_out.at[j, :, panel_span(n), :], chip_in.at[j, :, panel_span(4 + n), :],
            core_send.at[j, n], core_recv.at[j, n], at.to_core,
        )

    def contribute(j):
        sources = [at.near[j] * 4 + x * 2 + core for core in (1 - at.c, at.c) for x in (0, 1)]

        @pl.loop(0, 4)
        def _(n):
            span = panel_span(n)
            left = jnp.concatenate([slot_in[s, span, :] for s in sources], axis=0)
            for cols in tiles:
                value = product(left, weights[weight_span(n), cols]).astype(core_out.dtype)
                for x in (0, 1):
                    core_out[j, x, span, cols] = value[x * CAP : (x + 1) * CAP]
                    chip_in[j, x, span, cols] = value[(2 + x) * CAP : (3 + x) * CAP]
            core_copy(j, n).start()

    def spot(k):
        return 1 - at.second if k == 0 else at.second

    def combine(j):
        for n in range(4):
            core_copy(j, n).wait_recv()
        for kept in (False, True):
            for k in (0, 1):
                first = at.first if kept else 1 - at.first
                x = (1 - at.c) * spot(k) + at.c * first
                h = (1 - at.c) * first + at.c * spot(k)
                left = turned[2 * j + x, pl.ds(pl.multiple_of(h * half, half), half), :]
                for cols in tiles:
                    value = product(left, chip_in[j, x, :, cols])
                    if kept:
                        held[j, k, :, cols] = value
                    else:
                        first_out[j, k, :, cols] = value.astype(first_out.dtype)

    def first_copy(w, j, k):
        return remote(
            first_out.at[j, k, wave(w)], first_in.at[j, k, wave(w)], first_send.at[w, j, k], first_recv.at[w, j, k],
            at.to_first,
        )

    def second_copy(w, j):
        return remote(
            second_out.at[j, wave(w)], second_in.at[j, wave(w)], second_send.at[w, j], second_recv.at[w, j],
            at.to_second,
        )

    def z_arrived(w, slot):
        remote(
            z_in.at[slot, wave(w)], z_in.at[slot, wave(w)], z_send.at[w, 0], z_recv.at[w, slot], at.to_core
        ).wait_recv()

    def over_first(w, j):
        for k in (0, 1):
            first_copy(w, j, k).start()

    def over_second(w, j):
        first_copy(w, j, 0).wait_recv()
        second_out[j, wave(w)] = (held[j, 0, wave(w)] + f32(first_in[j, 0, wave(w)])).astype(second_out.dtype)
        second_copy(w, j).start()

    def along_z(w, j):
        rows = wave(w)
        first_copy(w, j, 1).wait_recv()
        second_copy(w, j).wait_recv()
        total = held[j, 1, rows] + f32(first_in[j, 1, rows]) + f32(second_in[j, rows])
        if j > 0:
            way = (at.z // 2) if j > 1 else (at.z % 2)
            slot = way * 4 + at.near[j]

            @pl.when(at.inner)
            def _():
                z_arrived(w, slot)
                z_out[j, rows] = (total + f32(z_in[slot, rows])).astype(z_out.dtype)

            @pl.when(jnp.logical_not(at.inner))
            def _():
                z_out[j, rows] = total.astype(z_out.dtype)

            remote(
                z_out.at[j, rows], z_in.at[slot, rows], z_send.at[w, j], z_recv.at[w, slot], at.along(1 - 2 * way)
            ).start()
        else:
            held[j, 1, rows] = total

            @pl.when(at.z > 0)
            def _():
                z_arrived(w, at.z)
                held[j, 1, rows] += f32(z_in[at.z, rows])

            @pl.when(at.z < 3)
            def _():
                z_arrived(w, 4 + at.z)
                held[j, 1, rows] += f32(z_in[4 + at.z, rows])

            error = f32(resid[rows]) - held[j, 1, rows]
            spread = jnp.mean(error * error, axis=-1, keepdims=True)
            grads[mine(0, False, False), rows] = (error * lax.rsqrt(spread + 1e-06)).astype(grads.dtype)
            spread_out(w)

    def block(z, first, second, core):
        return (z * 2 + core) * 4 + at.quarter(first, second)

    def mine(j, flip_first, flip_second):
        f = 1 - at.first if flip_first else at.first
        s = 1 - at.second if flip_second else at.second
        return block(at.near[j], f, s, at.c)

    def send(w, b, sem, target):
        remote(grads.at[b, wave(w)], grads.at[b, wave(w)], sem, block_recv.at[w, b], target).start()

    def arrived(w, b):
        remote(
            grads.at[b, wave(w)], grads.at[b, wave(w)], own_core.at[w, 0], block_recv.at[w, b], at.to_core
        ).wait_recv()

    used = [[0, 0, 0] for _ in range(WAVES)]

    def fan(w, b, second, first):
        if second:
            send(w, b, own_second.at[w, used[w][1]], at.to_second)
            used[w][1] += 1
        if first:
            send(w, b, own_first.at[w, used[w][0]], at.to_first)
            used[w][0] += 1
        send(w, b, own_core.at[w, used[w][2]], at.to_core)
        used[w][2] += 1

    def spread_out(w):
        b = mine(0, False, False)

        @pl.when(at.z > 0)
        def _():
            send(w, b, own_z.at[w, 0], at.along(-1))

        @pl.when(at.z < 3)
        def _():
            send(w, b, own_z.at[w, 1], at.along(1))

        fan(w, b, True, True)

    def from_z(w, j):
        b = mine(j, False, False)
        arrived(w, b)
        onward = (3 - 2 * at.z) if j == 1 else (2 * at.z - 3)

        @pl.when(at.inner)
        def _():
            send(w, b, own_z.at[w, 1 + j], at.along(onward))

        fan(w, b, True, True)

    def from_second(w, j):
        b = mine(j, False, True)
        arrived(w, b)
        fan(w, b, False, True)

    def from_first(w, j, flip):
        b = mine(j, True, flip)
        arrived(w, b)
        fan(w, b, False, False)

    def from_core(w, j):
        for q in range(4):
            arrived(w, (at.near[j] * 2 + 1 - at.c) * 4 + q)

    def slot_copy(target, source):
        return remote(
            slot_out.at[target], slot_back.at[source], slot_send.at[target], slot_recv.at[source], (target, at.y)
        )

    def pick(j, core):
        for x in (0, 1):
            source = at.near[j] * 4 + x * 2 + core
            rows = grads[pl.ds((at.near[j] * 2 + core) * 4 + 2 * x, 2)].reshape(tokens, width)
            for cols in tiles:
                value = product(hot[source, :slots, :], rows[:, cols]).astype(picked.dtype)
                for n in range(4):
                    picked[n, x * CAP : (x + 1) * CAP, cols] = value[n * CAP : (n + 1) * CAP]

    def project(j, core):
        pick(j, core)
        sources = [at.near[j] * 4 + x * 2 + core for x in (0, 1)]

        @pl.loop(0, 4)
        def _(n):
            span = panel_span(n)
            value = f32(product(picked[n], weights[weight_span(n), :], 1, 1).astype(jnp.bfloat16))
            value = value * f32(jnp.concatenate([slot_in[s, span, :] for s in sources], axis=0))
            high = value.astype(jnp.bfloat16)
            rest = (value - f32(high)).astype(jnp.bfloat16)
            for x in (0, 1):
                slot_out[sources[x], span, :] = high[x * CAP : (x + 1) * CAP]
                low[sources[x], span, :] = rest[x * CAP : (x + 1) * CAP]

        for source in sources:
            if j == 0:

                @pl.when(source != at.tok)
                def _():
                    slot_copy(source, at.tok).start()

            else:
                slot_copy(source, at.tok).start()

    unpack(0)
    load.wait()
    contribute(0)
    combine(0)
    for w in range(WAVES):
        over_first(w, 0)
    unpack(3)
    contribute(3)
    combine(3)
    over_first(0, 3)
    over_second(0, 0)
    unpack(2)
    contribute(2)
    combine(2)
    over_first(0, 2)
    over_second(0, 3)
    unpack(1)
    contribute(1)
    combine(1)
    over_first(0, 1)
    load_target.wait()
    over_first(1, 3)
    over_second(0, 2)
    along_z(0, 3)
    over_second(1, 0)
    over_first(1, 2)
    over_second(0, 1)
    along_z(0, 2)
    over_first(1, 1)
    along_z(0, 1)
    over_second(1, 3)
    along_z(0, 0)
    over_second(1, 2)
    along_z(1, 3)
    from_second(0, 0)
    from_z(0, 1)
    over_second(1, 1)
    along_z(1, 2)
    from_first(0, 0, False)
    from_second(0, 1)
    from_z(0, 2)
    along_z(1, 1)
    from_first(0, 0, True)
    from_first(0, 1, False)
    along_z(1, 0)
    from_second(0, 2)
    from_z(0, 3)
    from_first(0, 1, True)
    from_first(0, 2, False)
    from_second(0, 3)
    from_second(1, 0)
    from_z(1, 1)
    from_first(0, 2, True)
    from_first(0, 3, False)
    from_first(1, 0, False)
    from_second(1, 1)
    from_first(0, 3, True)
    from_z(1, 2)
    from_first(1, 0, True)
    for j in range(4):
        from_core(0, j)
    project(0, at.c)
    from_first(1, 1, False)
    from_second(1, 2)
    from_z(1, 3)
    from_first(1, 1, True)
    from_core(1, 0)
    project(0, 1 - at.c)
    project(1, at.c)
    from_first(1, 2, False)
    from_second(1, 3)
    from_core(1, 1)
    project(1, 1 - at.c)
    from_first(1, 2, True)
    project(2, at.c)
    from_first(1, 3, False)
    from_core(1, 2)
    project(2, 1 - at.c)
    from_first(1, 3, True)
    project(3, at.c)
    from_core(1, 3)
    project(3, 1 - at.c)

    slot_back[at.tok] = slot_out[at.tok]
    for n in range(4):
        span = slice(n * CAP, (n + 1) * CAP)
        asked = members[:, span, :].reshape(16 * CAP, tokens)
        total = product(asked, slot_out[:, span, :].reshape(16 * CAP, panel), 0, 0)
        total += product(asked, low[:, span, :].reshape(16 * CAP, panel), 0, 0)
        totals_ref[:, n * panel : (n + 1) * panel] = total[:REQUESTS]
    for distance in range(1, 16):
        source = (at.tok + distance) % 16
        slot_copy(source, source).wait_recv()
    for layer in (0, 1):
        table = slot_back[:, layer * 2 * CAP : (layer + 1) * 2 * CAP, :].reshape(32 * CAP, panel)
        for k in (0, 1):
            scores_ref[2 * layer + k] = product(sent[2 * layer + k], table, 0, 0).astype(scores_ref.dtype)

    for distance in range(1, 16):
        target = (at.tok + distance) % 16
        code_copy(target, target).wait_send()
        slot_copy(target, target).wait_send()
    for j in range(4):
        for n in range(4):
            core_copy(j, n).wait_send()
    for w in range(WAVES):
        sample = grads.at[0, wave(w)]

        def done(sem):
            remote(sample, sample, sem, block_recv.at[w, 0], at.to_core).wait_send()

        for j in range(4):
            first_copy(w, j, 0).wait_send()
            first_copy(w, j, 1).wait_send()
            second_copy(w, j).wait_send()
            if j > 0:
                done(z_send.at[w, j])
        for i in range(16):
            done(own_core.at[w, i])
        for i in range(8):
            done(own_first.at[w, i])
        for i in range(4):
            done(own_second.at[w, i])

        @pl.when(at.z > 0)
        def _():
            done(own_z.at[w, 0])

        @pl.when(at.z < 3)
        def _():
            done(own_z.at[w, 1])

        @pl.when(at.inner)
        def _():
            for i in range(2, 5):
                done(own_z.at[w, i])


def transcoder(codes, ids, requests, limits, weights, target):
    layers, tokens, panel = codes.shape
    depth, width = weights.shape
    half = target.shape[0] // 2
    step = half // WAVES
    dma, bf16 = pltpu.SemaphoreType.DMA, jnp.bfloat16
    vmem, anywhere = pl.BlockSpec(memory_space=pltpu.VMEM), pl.BlockSpec(memory_space=pl.ANY)
    slots = 4 * CAP

    def room(*shape, kind=bf16):
        return pltpu.VMEM(shape, kind)

    return pl.pallas_call(
        transcoder_kernel,
        out_shape=(
            jax.ShapeDtypeStruct((layers, tokens, panel), bf16),
            jax.ShapeDtypeStruct((REQUESTS, depth), jnp.float32),
        ),
        in_specs=[vmem] * 4 + [anywhere] * 2,
        out_specs=(vmem, vmem),
        scratch_shapes=[
            room(depth, width), room(half, width), room(16, slots + 16, panel), room(16, slots + 16, panel),
            room(4, 32 * CAP, tokens), room(16, 2 * slots, tokens), room(8, tokens, tokens), room(16, slots, tokens),
            room(4, 2, slots, width), room(4, 2, 2 * slots, width), room(4, 2, half, width, kind=jnp.float32),
            room(4, 2, half, width), room(4, 2, half, width), room(4, half, width), room(4, half, width),
            room(4, half, width), room(8, half, width), room(32, half, width), room(4, 2 * CAP, width),
            room(16, slots, panel), room(16, slots, panel), room(16, slots, panel),
            dma((2,)), dma((16,)), dma((16,)), dma((4, 4)), dma((4, 4)), dma((WAVES, 4, 2)), dma((WAVES, 4, 2)),
            dma((WAVES, 4)), dma((WAVES, 4)), dma((WAVES, 4)), dma((WAVES, 8)), dma((WAVES, 16)), dma((WAVES, 8)),
            dma((WAVES, 4)), dma((WAVES, 5)), dma((WAVES, 32)), dma((16,)), dma((16,)),
        ],
        compiler_params=pltpu.CompilerParams(
            collective_id=1, has_side_effects=True, vmem_limit_bytes=60 * 1024 * 1024
        ),
        name="transcoder",
    )(codes, ids, requests, limits, weights, target)


def per_device(feature_codes, block_ids, target_layer, request_ids, target_resid, decoder, grid=False):
    layers_here, count, kact, panel = feature_codes.shape
    width = target_resid.shape[1]
    features = decoder.shape[1]
    per_dev = features // panel
    tok, lyr = lax.axis_index("tok"), lax.axis_index("lyr")
    lyr_count = lax.axis_size("lyr")
    layer_ids = lyr * layers_here + jnp.arange(layers_here, dtype=jnp.int32)
    alive = layer_ids[:, None] <= target_layer[None, :]
    masked = jnp.where(alive[:, :, None, None], feature_codes, jnp.zeros_like(feature_codes))
    numbers = jnp.concatenate(
        [jnp.moveaxis(block_ids, 1, 2).reshape(layers_here * kact, count), request_ids[None, :]], axis=0
    )
    weights = decoder.reshape(layers_here * features, width)
    rows = count // lyr_count
    resid = lax.dynamic_slice_in_dim(target_resid, lyr * rows, rows, 0)
    if grid:
        by_k = jnp.moveaxis(feature_codes, 1, 2).reshape(layers_here * kact, count, panel)
        ids = jnp.moveaxis(block_ids, 1, 2).reshape(layers_here * kact, count)
        scores, totals = transcoder(by_k, ids, request_ids[None, :], target_layer[None, :], weights, target_resid)
        scores = jnp.moveaxis(scores.reshape(layers_here, kact, count, panel), 1, 2)
        return (scores, totals.reshape(REQUESTS, layers_here, features))
    all_codes = lax.all_gather(masked, "tok", axis=1, tiled=True)
    numbers = lax.all_gather(numbers, "tok", axis=1, tiled=True)
    all_ids = jnp.moveaxis(numbers[:-1].reshape(layers_here, kact, -1), 1, 2)
    all_requests = numbers[-1]
    mine = tok * per_dev + jnp.arange(per_dev, dtype=jnp.int32)
    named = (all_ids[..., None] == mine).astype(jnp.bfloat16)
    dense = jnp.sum(all_codes[:, :, :, None, :] * named[..., None], axis=2)
    tokens = dense.shape[1]
    dense = jnp.swapaxes(dense, 0, 1).reshape(tokens, layers_here * features)
    partial = jnp.dot(dense, weights, preferred_element_type=jnp.float32).astype(jnp.bfloat16)
    rebuilt = lax.psum_scatter(partial, ("tok", "lyr"), scatter_dimension=0, tiled=True)
    error = resid.astype(jnp.float32) - rebuilt.astype(jnp.float32)
    spread = jnp.mean(error * error, axis=-1, keepdims=True)
    gradient = (error * lax.rsqrt(spread + 1e-06)).astype(jnp.bfloat16)
    gradients = lax.all_gather(gradient, ("tok", "lyr"), axis=0, tiled=True)
    projected = lax.dot_general(
        gradients, weights, (((1,), (1,)), ((), ())), preferred_element_type=jnp.float32
    ).astype(jnp.bfloat16)
    attribution = dense.astype(jnp.float32) * projected.astype(jnp.float32)
    members = (all_requests[:, None] == jnp.arange(REQUESTS, dtype=jnp.int32)).astype(jnp.float32)
    totals = lax.dot_general(
        members, attribution, (((0,), (0,)), ((), ())), precision=lax.Precision.HIGHEST
    ).reshape(REQUESTS, layers_here, features)
    scored = attribution.astype(jnp.bfloat16).reshape(tokens, layers_here, 1, per_dev, panel)
    spread_out = jnp.sum(
        scored * jnp.swapaxes(named, 0, 1)[..., None], axis=3
    )
    scores = lax.psum_scatter(
        jnp.swapaxes(spread_out, 0, 1), "tok", scatter_dimension=1, tiled=True
    )
    return (scores, totals)


def solution(mesh):
    placed = (
        P("lyr", "tok", None, None),
        P("lyr", "tok", None),
        P("tok"),
        P("tok"),
        P("tok", None),
        P("lyr", "tok", None),
    )
    wide = len({getattr(d, "coords", (0,))[0] for d in mesh.devices.flat})
    grid = (mesh.shape["tok"], mesh.shape["lyr"]) == (16, 2) and wide == 2
    return jax.shard_map(
        functools.partial(per_device, grid=grid),
        mesh=mesh,
        in_specs=placed,
        out_specs=(P("lyr", "tok", None, None), P(None, "lyr", "tok")),
        check_vma=False,
    )
```

```python
import functools

import jax
import jax.numpy as jnp
from jax import lax
from jax.experimental import pallas as pl
from jax.experimental.pallas import tpu as pltpu
from jax.sharding import PartitionSpec as P

REQUESTS = 16
CAP = 16
MESH = pl.DeviceIdType.MESH


WAVES = ((0, 32, False), (32, 16, True), (48, 8, False))
LAST = (56, 8)


class Route:
    def __init__(self, at, c):
        x, y, self.c = at.x, at.y, c
        self.first = (1 - c) * y + c * x
        self.second = (1 - c) * x + c * y
        across_x, across_y = (at.tok + 2 - 4 * x, y), (at.tok, 1 - y)
        self.to_first = tuple((1 - c) * a + c * b for a, b in zip(across_y, across_x))
        self.to_second = tuple((1 - c) * a + c * b for a, b in zip(across_x, across_y))

    def spot(self, flip_first, flip_second):
        f = 1 - self.first if flip_first else self.first
        s = 1 - self.second if flip_second else self.second
        return (1 - self.c) * s + self.c * f, (1 - self.c) * f + self.c * s


class Place:
    def __init__(self):
        tok, y = lax.axis_index("tok"), lax.axis_index("lyr")
        z, x, c = tok // 4, (tok // 2) % 2, tok % 2
        self.z, self.x, self.c = z, x, c
        self.inner = (z % 3) != 0
        self.to_core = (tok + 1 - 2 * c, y)
        self.tok, self.y = tok, y
        half = z // 2
        self.near = [z, z + 1 - 2 * (z % 2), 2 - half, 3 - 3 * half]

    def along(self, step):
        return (self.tok + 4 * step, self.y)

    def peer(self, distance):
        return ((self.tok + distance) % 16, self.y)

    def greet(self):
        gate = pltpu.get_barrier_semaphore()
        for distance in range(1, 16):
            pl.semaphore_signal(gate, inc=1, device_id=self.peer(distance), device_id_type=MESH)
        pl.semaphore_signal(gate, inc=1, device_id=(self.tok, 1 - self.y), device_id_type=MESH)

    def meet(self):
        pl.semaphore_wait(pltpu.get_barrier_semaphore(), 16)


def remote(src, dst, send, recv, target):
    return pltpu.make_async_remote_copy(
        src_ref=src, dst_ref=dst, send_sem=send, recv_sem=recv, device_id=target, device_id_type=MESH
    )


def f32(value):
    return value.astype(jnp.float32)


def ones(where):
    return jnp.where(where, 1.0, 0.0).astype(jnp.bfloat16)


def rows_of(shape):
    return lax.broadcasted_iota(jnp.int32, shape, 0)


def lanes_of(shape):
    return lax.broadcasted_iota(jnp.int32, shape, 1)


def product(left, right, left_dim=1, right_dim=0):
    return lax.dot_general(left, right, (((left_dim,), (right_dim,)), ((), ())), preferred_element_type=jnp.float32)


def transcoder_kernel(
    codes_ref, ids_ref, request_ref, limit_ref, decoder_ref, target_ref, scores_ref, totals_ref,
    weights, resid, packed, slot_in, sent, hot, turned, members, core_out, chip_in, held, final,
    first_out, first_in, second_out, second_in, z_out, z_in, grads, picked, slot_out, slot_back, low,
    last_total, last_first_out, last_first_in, last_second_out, last_second_in, last_out, last_in,
    load_sem, code_send, code_recv, core_send, core_recv, first_send, first_recv, second_send, second_recv,
    z_send, z_recv, own_core, own_first, own_second, own_z, block_recv, slot_send, slot_recv, last_send, last_recv,
):
    at = Place()
    at.greet()
    half, width = resid.shape
    tokens = limit_ref.shape[1]
    panel = codes_ref.shape[-1]
    slots = 4 * CAP
    routes = [Route(at, 0 if flipped else at.c) for _, _, flipped in WAVES]
    tile = width // 3 if width % 384 == 0 else width
    tiles = [slice(t, t + tile) for t in range(0, width, tile)]
    load = pltpu.make_async_copy(decoder_ref, weights, load_sem.at[0])
    load.start()
    load_target = pltpu.make_async_copy(
        target_ref.at[pl.ds(pl.multiple_of(at.y * half, half), half)], resid, load_sem.at[1]
    )
    load_target.start()

    def wave(w):
        return pl.ds(WAVES[w][0], WAVES[w][1])

    info = []
    ids = ids_ref[...]
    shape = (tokens, tokens)
    earlier = ones(rows_of(shape) < lanes_of(shape))
    panels = rows_of((32, tokens))
    numbers = []
    for layer in (0, 1):
        named = [ids[2 * layer + k : 2 * layer + k + 1] == panels for k in (0, 1)]
        before = product(ones(named[0] | named[1]), earlier)
        alive = limit_ref[...] >= 2 * at.y + layer
        value = None
        for k in (0, 1):
            rank = jnp.sum(jnp.where(named[k], before, 0.0), axis=0, keepdims=True)
            number = f32(ids[2 * layer + k : 2 * layer + k + 1])
            numbers.append((number, rank))
            code = jnp.where(alive, number * CAP + rank, -1.0)
            spot = ones(f32(rows_of((32 * CAP, tokens))) == code)
            sent[2 * layer + k] = spot
            part = product(spot, codes_ref[2 * layer + k])
            value = part if value is None else value + part
        packed[:, layer * 2 * CAP : (layer + 1) * 2 * CAP, :] = value.astype(packed.dtype).reshape(16, 2 * CAP, panel)
    blank = jnp.zeros((7, tokens), jnp.float32)
    info = jnp.concatenate(
        [n for n, _ in numbers] + [r for _, r in numbers] + [f32(request_ref[...]), blank], axis=0
    )
    info = jnp.concatenate([info] * (panel // tokens), axis=1).astype(packed.dtype)
    for target in range(16):
        packed[target, slots : slots + 16, :] = info
    slot_in[at.tok] = packed[at.tok]
    order = (0, 3, 2, 1)

    def peers(j):
        return [at.near[j] * 4 + (at.tok + s) % 4 for s in range(1 if j == 0 else 0, 4)]

    def code_copy(target, source):
        return remote(packed.at[target], slot_in.at[source], code_send.at[target], code_recv.at[source], (target, at.y))

    at.meet()
    for j in order:
        for target in peers(j):
            code_copy(target, at.tok).start()

    eye = ones(rows_of(shape) == lanes_of(shape))

    def unpack(j):
        for source in peers(j):
            code_copy(source, source).wait_recv()

        @pl.loop(0, 4)
        def _(s):
            source = at.near[j] * 4 + s
            told = f32(slot_in[source, slots : slots + 16, :tokens])
            place = [told[i : i + 1] * CAP + told[4 + i : 5 + i] for i in range(4)]
            for away in (0, 1):
                device = at.tok if away == 0 else at.tok + 1 - 2 * at.c
                row = f32(rows_of((2 * CAP, tokens)) + device * (2 * CAP))
                for layer in (0, 1):
                    start = away * slots + layer * 2 * CAP
                    hot[source, start : start + 2 * CAP, :] = ones(
                        (place[2 * layer] == row) | (place[2 * layer + 1] == row)
                    )
            asks = ones(f32(rows_of(shape)) == told[8:9])
            members[source] = product(hot[source, :slots, :], asks, 1, 1).astype(members.dtype)

        for x in (0, 1):
            source = at.near[j] * 4 + x * 2 + at.c
            turned[2 * j + x] = product(hot[source], eye, 0, 0).astype(turned.dtype)

    def panel_span(n):
        return pl.ds(pl.multiple_of(n * CAP, CAP), CAP)

    def weight_span(n):
        return pl.ds(pl.multiple_of(n * panel, panel), panel)

    def core_copy(j, n):
        return remote(
            core_out.at[j, :, panel_span(n), :], chip_in.at[j, :, panel_span(4 + n), :],
            core_send.at[j, n], core_recv.at[j, n], at.to_core,
        )

    def contribute(j):
        sources = [at.near[j] * 4 + x * 2 + core for core in (1 - at.c, at.c) for x in (0, 1)]

        @pl.loop(0, 4)
        def _(n):
            span = panel_span(n)
            left = jnp.concatenate([slot_in[s, span, :] for s in sources], axis=0)
            for cols in tiles:
                value = product(left, weights[weight_span(n), cols]).astype(core_out.dtype)
                for x in (0, 1):
                    core_out[j, x, span, cols] = value[x * CAP : (x + 1) * CAP]
                    chip_in[j, x, span, cols] = value[(2 + x) * CAP : (3 + x) * CAP]
            core_copy(j, n).start()

    def combine(j):
        for n in range(4):
            core_copy(j, n).wait_recv()
        for x in (0, 1):
            for cols in tiles:
                held[j, x, :, cols] = product(turned[2 * j + x], chip_in[j, x, :, cols])

    def kept(w, j, flip_first, flip_second):
        x, h = routes[w].spot(flip_first, flip_second)
        return held[j, x, pl.ds(pl.multiple_of(h * half + WAVES[w][0], 8), WAVES[w][1])]

    def first_copy(w, j, k):
        return remote(
            first_out.at[j, k, wave(w)], first_in.at[j, k, wave(w)], first_send.at[w, j, k], first_recv.at[w, j, k],
            routes[w].to_first,
        )

    def second_copy(w, j):
        return remote(
            second_out.at[j, wave(w)], second_in.at[j, wave(w)], second_send.at[w, j], second_recv.at[w, j],
            routes[w].to_second,
        )

    def z_arrived(w, slot):
        remote(
            z_in.at[slot, wave(w)], z_in.at[slot, wave(w)], z_send.at[w, 0], z_recv.at[w, slot], at.to_core
        ).wait_recv()

    def over_first(w, j):
        for k in (0, 1):
            first_out[j, k, wave(w)] = kept(w, j, True, k == 0).astype(first_out.dtype)
            first_copy(w, j, k).start()

    def over_second(w, j):
        first_copy(w, j, 0).wait_recv()
        second_out[j, wave(w)] = (kept(w, j, False, True) + f32(first_in[j, 0, wave(w)])).astype(second_out.dtype)
        second_copy(w, j).start()

    def along_z(w, j):
        rows = wave(w)
        first_copy(w, j, 1).wait_recv()
        second_copy(w, j).wait_recv()
        total = kept(w, j, False, False) + f32(first_in[j, 1, rows]) + f32(second_in[j, rows])
        if j > 0:
            way = (at.z // 2) if j > 1 else (at.z % 2)
            slot = way * 4 + at.near[j]

            @pl.when(at.inner)
            def _():
                z_arrived(w, slot)
                z_out[j, rows] = (total + f32(z_in[slot, rows])).astype(z_out.dtype)

            @pl.when(jnp.logical_not(at.inner))
            def _():
                z_out[j, rows] = total.astype(z_out.dtype)

            remote(
                z_out.at[j, rows], z_in.at[slot, rows], z_send.at[w, j], z_recv.at[w, slot], at.along(1 - 2 * way)
            ).start()
        else:
            final[rows] = total

            @pl.when(at.z > 0)
            def _():
                z_arrived(w, at.z)
                final[rows] += f32(z_in[at.z, rows])

            @pl.when(at.z < 3)
            def _():
                z_arrived(w, 4 + at.z)
                final[rows] += f32(z_in[4 + at.z, rows])

            grads[mine(w, 0, False, False), rows] = gradient(rows, final[rows])
            spread_out(w)

    def gradient(rows, rebuilt):
        error = f32(resid[rows]) - rebuilt
        spread = jnp.mean(error * error, axis=-1, keepdims=True)
        return (error * lax.rsqrt(spread + 1e-06)).astype(grads.dtype)

    def mine(w, j, flip_first, flip_second):
        x, h = routes[w].spot(flip_first, flip_second)
        return (at.near[j] * 2 + at.c) * 4 + x * 2 + h

    def send(w, b, sem, target):
        remote(grads.at[b, wave(w)], grads.at[b, wave(w)], sem, block_recv.at[w, b], target).start()

    def arrived(w, b):
        remote(
            grads.at[b, wave(w)], grads.at[b, wave(w)], own_core.at[w, 0], block_recv.at[w, b], at.to_core
        ).wait_recv()

    used = [[0, 0, 0] for _ in WAVES]

    def fan(w, b, second, first):
        if second:
            send(w, b, own_second.at[w, used[w][1]], routes[w].to_second)
            used[w][1] += 1
        if first:
            send(w, b, own_first.at[w, used[w][0]], routes[w].to_first)
            used[w][0] += 1
        send(w, b, own_core.at[w, used[w][2]], at.to_core)
        used[w][2] += 1

    def spread_out(w):
        b = mine(w, 0, False, False)

        @pl.when(at.z > 0)
        def _():
            send(w, b, own_z.at[w, 0], at.along(-1))

        @pl.when(at.z < 3)
        def _():
            send(w, b, own_z.at[w, 1], at.along(1))

        fan(w, b, True, True)

    def from_z(w, j):
        b = mine(w, j, False, False)
        arrived(w, b)
        onward = (3 - 2 * at.z) if j == 1 else (2 * at.z - 3)

        @pl.when(at.inner)
        def _():
            send(w, b, own_z.at[w, 1 + j], at.along(onward))

        fan(w, b, True, True)

    def from_second(w, j):
        b = mine(w, j, False, True)
        arrived(w, b)
        fan(w, b, False, True)

    def from_first(w, j, flip):
        b = mine(w, j, True, flip)
        arrived(w, b)
        fan(w, b, False, False)

    def from_core(w, j):
        for q in range(4):
            arrived(w, (at.near[j] * 2 + 1 - at.c) * 4 + q)

    last = pl.ds(LAST[0], LAST[1])
    route = Route(at, at.c)

    def last_held(j, x, h):
        return held[j, x, pl.ds(pl.multiple_of(h * half + LAST[0], 8), LAST[1])]

    def last_along(way, slot, j, step):
        return remote(last_out.at[j], last_in.at[slot], last_send.at[j], last_recv.at[slot], at.along(step))

    def last_quarter(flip_first, flip_second):
        x, h = route.spot(flip_first, flip_second)
        return x * 2 + h

    def last_over_first():
        return remote(last_first_out, last_first_in, last_send.at[4], last_recv.at[8], route.to_first)

    def last_over_second():
        return remote(last_second_out, last_second_in, last_send.at[5], last_recv.at[9], route.to_second)

    def last_z(j):
        def come(slot):
            remote(last_in.at[slot], last_in.at[slot], last_send.at[0], last_recv.at[slot], at.to_core).wait_recv()

        if j > 0:
            way = (at.z // 2) if j > 1 else (at.z % 2)
            slot = way * 4 + at.near[j]

            @pl.when(at.inner)
            def _():
                come(slot)
                for q in range(4):
                    last_out[j, q] = (last_held(j, q // 2, q % 2) + f32(last_in[slot, q])).astype(last_out.dtype)

            @pl.when(jnp.logical_not(at.inner))
            def _():
                for q in range(4):
                    last_out[j, q] = last_held(j, q // 2, q % 2).astype(last_out.dtype)

            last_along(way, slot, j, 1 - 2 * way).start()
        else:
            for q in range(4):
                last_total[q] = last_held(0, q // 2, q % 2)

            @pl.when(at.z > 0)
            def _():
                come(at.z)
                for q in range(4):
                    last_total[q] += f32(last_in[at.z, q])

            @pl.when(at.z < 3)
            def _():
                come(4 + at.z)
                for q in range(4):
                    last_total[q] += f32(last_in[4 + at.z, q])

            for k in (0, 1):
                last_first_out[k] = last_total[last_quarter(True, k == 0)].astype(last_out.dtype)
            last_over_first().start()

    def last_second():
        last_over_first().wait_recv()
        last_second_out[...] = (last_total[last_quarter(False, True)] + f32(last_first_in[0])).astype(last_out.dtype)
        last_over_second().start()

    def last_group(plane, core):
        return grads.at[pl.ds((plane * 2 + core) * 4, 4), last]

    def last_block(flip_first, flip_second):
        return grads.at[(at.z * 2 + at.c) * 4 + last_quarter(flip_first, flip_second), last]

    def last_pass(ref, sem, arrival, target):
        return remote(ref, ref, last_send.at[sem], last_recv.at[arrival], target)

    def last_final():
        last_over_second().wait_recv()
        total = last_total[last_quarter(False, False)] + f32(last_first_in[1]) + f32(last_second_in[...])
        grads[(at.z * 2 + at.c) * 4 + last_quarter(False, False), last] = gradient(last, total)
        own = last_block(False, False)
        last_pass(own, 6, 10, route.to_second).start()
        last_pass(own, 7, 11, route.to_first).start()

    def last_from_second():
        ref = last_block(False, True)
        last_pass(ref, 6, 10, at.to_core).wait_recv()
        last_pass(ref, 8, 12, route.to_first).start()

    def last_from_first():
        last_pass(last_block(True, False), 6, 11, at.to_core).wait_recv()
        last_pass(last_block(True, True), 6, 12, at.to_core).wait_recv()
        ref = last_group(at.z, at.c)

        @pl.when(at.z > 0)
        def _():
            last_pass(ref, 9, 13 + at.z, at.along(-1)).start()

        @pl.when(at.z < 3)
        def _():
            last_pass(ref, 10, 13 + at.z, at.along(1)).start()

        last_pass(ref, 14, 17 + at.z, at.to_core).start()

    def last_from_z(j):
        ref = last_group(at.near[j], at.c)
        last_pass(ref, 6, 13 + at.near[j], at.to_core).wait_recv()
        onward = (3 - 2 * at.z) if j == 1 else (2 * at.z - 3)

        @pl.when(at.inner)
        def _():
            last_pass(ref, 10 + j, 13 + at.near[j], at.along(onward)).start()

        last_pass(ref, 14 + j, 17 + at.near[j], at.to_core).start()

    def last_from_core(j):
        last_pass(last_group(at.near[j], 1 - at.c), 6, 17 + at.near[j], at.to_core).wait_recv()

    def slot_copy(target, source):
        return remote(
            slot_out.at[target], slot_back.at[source], slot_send.at[target], slot_recv.at[source], (target, at.y)
        )

    def place_of(j, core):
        return [at.near[j] * 4 + x * 2 + core for x in (0, 1)]

    def pick(j, away):
        core = 1 - at.c if away else at.c
        for x, source in enumerate(place_of(j, core)):
            rows = grads[pl.ds((at.near[j] * 2 + core) * 4 + 2 * x, 2)].reshape(tokens, width)
            start = (2 * away + x) * CAP
            for cols in tiles:
                value = product(hot[source, :slots, :], rows[:, cols]).astype(picked.dtype)
                for n in range(4):
                    picked[n, start : start + CAP, cols] = value[n * CAP : (n + 1) * CAP]

    def project(j):
        sources = place_of(j, at.c) + place_of(j, 1 - at.c)

        @pl.loop(0, 4)
        def _(n):
            span = panel_span(n)
            value = f32(product(picked[n], weights[weight_span(n), :], 1, 1).astype(jnp.bfloat16))
            value = value * f32(jnp.concatenate([slot_in[s, span, :] for s in sources], axis=0))
            high = value.astype(jnp.bfloat16)
            rest = (value - f32(high)).astype(jnp.bfloat16)
            for i, source in enumerate(sources):
                slot_out[source, span, :] = high[i * CAP : (i + 1) * CAP]
                low[source, span, :] = rest[i * CAP : (i + 1) * CAP]

        for i, source in enumerate(sources):
            if j == 0 and i < 2:

                @pl.when(source != at.tok)
                def _():
                    slot_copy(source, at.tok).start()

            else:
                slot_copy(source, at.tok).start()

    unpack(0)
    load.wait()
    contribute(0)
    combine(0)
    over_first(0, 0)
    over_first(1, 0)
    unpack(3)
    contribute(3)
    combine(3)
    over_first(0, 3)
    last_z(3)
    over_second(0, 0)
    unpack(2)
    contribute(2)
    combine(2)
    over_first(0, 2)
    last_z(2)
    over_second(0, 3)
    unpack(1)
    contribute(1)
    combine(1)
    over_first(0, 1)
    last_z(1)
    over_second(1, 0)
    over_second(0, 2)
    along_z(0, 3)
    over_first(1, 3)
    over_second(0, 1)
    along_z(0, 2)
    over_first(1, 2)
    last_z(0)
    along_z(0, 1)
    over_second(1, 3)
    over_first(1, 1)
    last_second()
    over_first(2, 0)
    over_first(2, 3)
    load_target.wait()
    along_z(0, 0)
    over_second(1, 2)
    last_final()
    along_z(1, 3)
    over_first(2, 2)
    over_first(2, 1)
    over_second(1, 1)
    along_z(1, 2)
    over_second(2, 0)
    over_second(2, 3)
    from_second(0, 0)
    from_z(0, 1)
    last_from_second()
    along_z(1, 1)
    over_second(2, 2)
    along_z(2, 3)
    from_first(0, 0, False)
    from_second(0, 1)
    from_z(0, 2)
    along_z(1, 0)
    over_second(2, 1)
    along_z(2, 2)
    last_from_first()
    from_first(0, 0, True)
    from_first(0, 1, False)
    from_second(0, 2)
    from_z(0, 3)
    along_z(2, 1)
    along_z(2, 0)
    from_second(1, 0)
    from_z(1, 1)
    from_first(0, 1, True)
    from_first(0, 2, False)
    from_second(0, 3)
    last_from_z(1)
    from_z(1, 2)
    from_second(1, 1)
    from_first(0, 2, True)
    from_first(0, 3, False)
    from_second(2, 0)
    from_z(2, 1)
    from_first(1, 0, False)
    last_from_z(2)
    from_z(1, 3)
    from_second(1, 2)
    from_first(0, 3, True)
    from_first(1, 0, True)
    from_second(2, 1)
    from_z(2, 2)
    last_from_z(3)
    from_first(1, 1, False)
    from_second(1, 3)
    from_first(1, 1, True)
    from_z(2, 3)
    from_second(2, 2)
    from_first(1, 2, False)
    from_first(2, 0, False)
    from_first(2, 0, True)
    from_first(1, 2, True)
    from_second(2, 3)
    from_core(0, 0)
    from_core(1, 0)
    from_core(2, 0)
    last_from_core(0)
    pick(0, False)
    pick(0, True)
    from_first(1, 3, False)
    from_first(1, 3, True)
    from_first(2, 1, False)
    project(0)
    from_first(2, 1, True)
    from_first(2, 2, False)
    from_first(2, 2, True)
    from_core(0, 1)
    from_core(1, 1)
    from_core(2, 1)
    last_from_core(1)
    pick(1, False)
    pick(1, True)
    from_first(2, 3, False)
    from_first(2, 3, True)
    project(1)
    from_core(0, 2)
    from_core(1, 2)
    from_core(2, 2)
    last_from_core(2)
    pick(2, False)
    pick(2, True)
    project(2)
    pick(3, False)
    from_core(0, 3)
    from_core(1, 3)
    from_core(2, 3)
    last_from_core(3)
    pick(3, True)
    project(3)

    slot_back[at.tok] = slot_out[at.tok]
    for n in range(4):
        span = slice(n * CAP, (n + 1) * CAP)
        asked = members[:, span, :].reshape(16 * CAP, tokens)
        total = product(asked, slot_out[:, span, :].reshape(16 * CAP, panel), 0, 0)
        total += product(asked, low[:, span, :].reshape(16 * CAP, panel), 0, 0)
        totals_ref[:, n * panel : (n + 1) * panel] = total[:REQUESTS]
    for distance in range(1, 16):
        source = (at.tok + distance) % 16
        slot_copy(source, source).wait_recv()
    for layer in (0, 1):
        table = slot_back[:, layer * 2 * CAP : (layer + 1) * 2 * CAP, :].reshape(32 * CAP, panel)
        for k in (0, 1):
            scores_ref[2 * layer + k] = product(sent[2 * layer + k], table, 0, 0).astype(scores_ref.dtype)

    for distance in range(1, 16):
        target = (at.tok + distance) % 16
        code_copy(target, target).wait_send()
        slot_copy(target, target).wait_send()
    for j in range(4):
        for n in range(4):
            core_copy(j, n).wait_send()
    for w in range(len(WAVES)):
        sample = grads.at[0, wave(w)]

        def done(sem):
            remote(sample, sample, sem, block_recv.at[w, 0], at.to_core).wait_send()

        for j in range(4):
            first_copy(w, j, 0).wait_send()
            first_copy(w, j, 1).wait_send()
            second_copy(w, j).wait_send()
            if j > 0:
                done(z_send.at[w, j])
        for i in range(16):
            done(own_core.at[w, i])
        for i in range(8):
            done(own_first.at[w, i])
        for i in range(4):
            done(own_second.at[w, i])

        @pl.when(at.z > 0)
        def _():
            done(own_z.at[w, 0])

        @pl.when(at.z < 3)
        def _():
            done(own_z.at[w, 1])

        @pl.when(at.inner)
        def _():
            for i in range(2, 5):
                done(own_z.at[w, i])


    last_over_first().wait_send()
    last_over_second().wait_send()
    for j in range(1, 4):
        last_pass(last_out.at[j], j, 0, at.to_core).wait_send()
    one, four = last_block(False, False), last_group(at.z, at.c)
    for i in (6, 7, 8):
        last_pass(one, i, 10, at.to_core).wait_send()
    for i in range(14, 18):
        last_pass(four, i, 10, at.to_core).wait_send()

    @pl.when(at.z > 0)
    def _():
        last_pass(four, 9, 10, at.to_core).wait_send()

    @pl.when(at.z < 3)
    def _():
        last_pass(four, 10, 10, at.to_core).wait_send()

    @pl.when(at.inner)
    def _():
        for i in range(11, 14):
            last_pass(four, i, 10, at.to_core).wait_send()


def transcoder(codes, ids, requests, limits, weights, target):
    layers, tokens, panel = codes.shape
    depth, width = weights.shape
    half = target.shape[0] // 2
    waves, quick = len(WAVES), LAST[1]
    dma, bf16 = pltpu.SemaphoreType.DMA, jnp.bfloat16
    vmem, anywhere = pl.BlockSpec(memory_space=pltpu.VMEM), pl.BlockSpec(memory_space=pl.ANY)
    slots = 4 * CAP

    def room(*shape, kind=bf16):
        return pltpu.VMEM(shape, kind)

    return pl.pallas_call(
        transcoder_kernel,
        out_shape=(
            jax.ShapeDtypeStruct((layers, tokens, panel), bf16),
            jax.ShapeDtypeStruct((REQUESTS, depth), jnp.float32),
        ),
        in_specs=[vmem] * 4 + [anywhere] * 2,
        out_specs=(vmem, vmem),
        scratch_shapes=[
            room(depth, width), room(half, width), room(16, slots + 16, panel), room(16, slots + 16, panel),
            room(4, 32 * CAP, tokens), room(16, 2 * slots, tokens), room(8, tokens, tokens), room(16, slots, tokens),
            room(4, 2, slots, width), room(4, 2, 2 * slots, width), room(4, 2, tokens, width, kind=jnp.float32),
            room(half, width, kind=jnp.float32), room(4, 2, half, width), room(4, 2, half, width), room(4, half, width), room(4, half, width),
            room(4, half, width), room(8, half, width), room(32, half, width), room(4, 4 * CAP, width),
            room(16, slots, panel), room(16, slots, panel), room(16, slots, panel),
            room(4, quick, width, kind=jnp.float32), room(2, quick, width), room(2, quick, width), room(quick, width),
            room(quick, width), room(4, 4, quick, width), room(8, 4, quick, width),
            dma((2,)), dma((16,)), dma((16,)), dma((4, 4)), dma((4, 4)), dma((waves, 4, 2)), dma((waves, 4, 2)),
            dma((waves, 4)), dma((waves, 4)), dma((waves, 4)), dma((waves, 8)), dma((waves, 16)), dma((waves, 8)),
            dma((waves, 4)), dma((waves, 5)), dma((waves, 32)), dma((16,)), dma((16,)),
            dma((18,)), dma((21,)),
        ],
        compiler_params=pltpu.CompilerParams(
            collective_id=1, has_side_effects=True, vmem_limit_bytes=60 * 1024 * 1024
        ),
        name="transcoder",
    )(codes, ids, requests, limits, weights, target)


def per_device(feature_codes, block_ids, target_layer, request_ids, target_resid, decoder, grid=False):
    layers_here, count, kact, panel = feature_codes.shape
    width = target_resid.shape[1]
    features = decoder.shape[1]
    per_dev = features // panel
    tok, lyr = lax.axis_index("tok"), lax.axis_index("lyr")
    lyr_count = lax.axis_size("lyr")
    layer_ids = lyr * layers_here + jnp.arange(layers_here, dtype=jnp.int32)
    alive = layer_ids[:, None] <= target_layer[None, :]
    masked = jnp.where(alive[:, :, None, None], feature_codes, jnp.zeros_like(feature_codes))
    numbers = jnp.concatenate(
        [jnp.moveaxis(block_ids, 1, 2).reshape(layers_here * kact, count), request_ids[None, :]], axis=0
    )
    weights = decoder.reshape(layers_here * features, width)
    rows = count // lyr_count
    resid = lax.dynamic_slice_in_dim(target_resid, lyr * rows, rows, 0)
    if grid:
        by_k = jnp.moveaxis(feature_codes, 1, 2).reshape(layers_here * kact, count, panel)
        ids = jnp.moveaxis(block_ids, 1, 2).reshape(layers_here * kact, count)
        scores, totals = transcoder(by_k, ids, request_ids[None, :], target_layer[None, :], weights, target_resid)
        scores = jnp.moveaxis(scores.reshape(layers_here, kact, count, panel), 1, 2)
        return (scores, totals.reshape(REQUESTS, layers_here, features))
    all_codes = lax.all_gather(masked, "tok", axis=1, tiled=True)
    numbers = lax.all_gather(numbers, "tok", axis=1, tiled=True)
    all_ids = jnp.moveaxis(numbers[:-1].reshape(layers_here, kact, -1), 1, 2)
    all_requests = numbers[-1]
    mine = tok * per_dev + jnp.arange(per_dev, dtype=jnp.int32)
    named = (all_ids[..., None] == mine).astype(jnp.bfloat16)
    dense = jnp.sum(all_codes[:, :, :, None, :] * named[..., None], axis=2)
    tokens = dense.shape[1]
    dense = jnp.swapaxes(dense, 0, 1).reshape(tokens, layers_here * features)
    partial = jnp.dot(dense, weights, preferred_element_type=jnp.float32).astype(jnp.bfloat16)
    rebuilt = lax.psum_scatter(partial, ("tok", "lyr"), scatter_dimension=0, tiled=True)
    error = resid.astype(jnp.float32) - rebuilt.astype(jnp.float32)
    spread = jnp.mean(error * error, axis=-1, keepdims=True)
    gradient = (error * lax.rsqrt(spread + 1e-06)).astype(jnp.bfloat16)
    gradients = lax.all_gather(gradient, ("tok", "lyr"), axis=0, tiled=True)
    projected = lax.dot_general(
        gradients, weights, (((1,), (1,)), ((), ())), preferred_element_type=jnp.float32
    ).astype(jnp.bfloat16)
    attribution = dense.astype(jnp.float32) * projected.astype(jnp.float32)
    members = (all_requests[:, None] == jnp.arange(REQUESTS, dtype=jnp.int32)).astype(jnp.float32)
    totals = lax.dot_general(
        members, attribution, (((0,), (0,)), ((), ())), precision=lax.Precision.HIGHEST
    ).reshape(REQUESTS, layers_here, features)
    scored = attribution.astype(jnp.bfloat16).reshape(tokens, layers_here, 1, per_dev, panel)
    spread_out = jnp.sum(
        scored * jnp.swapaxes(named, 0, 1)[..., None], axis=3
    )
    scores = lax.psum_scatter(
        jnp.swapaxes(spread_out, 0, 1), "tok", scatter_dimension=1, tiled=True
    )
    return (scores, totals)


def solution(mesh):
    placed = (
        P("lyr", "tok", None, None),
        P("lyr", "tok", None),
        P("tok"),
        P("tok"),
        P("tok", None),
        P("lyr", "tok", None),
    )
    wide = len({getattr(d, "coords", (0,))[0] for d in mesh.devices.flat})
    grid = (mesh.shape["tok"], mesh.shape["lyr"]) == (16, 2) and wide == 2
    return jax.shard_map(
        functools.partial(per_device, grid=grid),
        mesh=mesh,
        in_specs=placed,
        out_specs=(P("lyr", "tok", None, None), P(None, "lyr", "tok")),
        check_vma=False,
    )
```
